32 devices in a mesh: dp: 4 (over y, x), tensor: 8 (over z, core).
Axes of the slice: x: 2, y: 2, z: 4, core: 2. Of those that a mesh axis runs over, the one named last changes fastest.
Arguments:
- hidden_in: bfloat16 [8192, 2048], P(('dp', 'tensor')), parts along dimension 0, may hold values from -6 to 6
- attn_gain: float32 [2048], replicated, may hold values from 0.1 to 1.9
- attn_shift: float32 [2048], replicated, may hold values from -3 to 3
- qkv_weight: bfloat16 [2048, 6144], P(None, 'tensor'), may hold values from -4 to 4
- qkv_bias: bfloat16 [6144], P('tensor'), may hold values from -3 to 3
- out_weight: bfloat16 [2048, 2048], P('tensor'), may hold values from -0.125 to 0.125
- out_bias: float32 [2048], replicated, may hold values from -3 to 3
- mlp_gain: float32 [2048], replicated, may hold values from 0.1 to 1.9
- mlp_shift: float32 [2048], replicated, may hold values from -3 to 3
- up_weight: bfloat16 [2048, 8192], P(None, 'tensor'), may hold values from -0.125 to 0.125
- up_bias: float32 [8192], P('tensor'), may hold values from -3 to 3
- down_weight: bfloat16 [8192, 2048], P('tensor'), may hold values from -0.0625 to 0.0625
- down_bias: float32 [2048], replicated, may hold values from -3 to 3
- segment_ids: int32 [4, 2048], P('dp'), parts along dimension 0, may hold values from 0 to 7, never falling along the last dimension, each value on 1 to 1024 neighbouring positions
- prompt_lengths: int32 [4], P('dp'), parts along dimension 0, may hold values from 1024 to 2048
- page_table: int32 [512, 1], P('dp'), parts along dimension 0, may hold values from 0 to 7; in each aligned block of 128 rows (0 to 127, 128 to 255, ...) at most 32 rows name the same one
Outputs:
- layer_out: bfloat16 [8192, 2048], P(('dp', 'tensor')), parts along dimension 0
- kv_pages: bfloat16 [1024, 16, 4096], P(('dp', 'tensor')), parts along dimension 0
The draws below stay inside these ranges and needn't reach their ends.
There are 4 independent parts, one for each index of `dp`. The reference program is written for one: setup_inputs(seed, part) draws one part's arguments, and reference() takes and returns one part's arrays. A program takes and returns all parts, laid end to end along the dimension named above; an argument that names none is the same for every part. Nothing has to cross between parts.
Inputs may be any that keep to these rules, and one draw needn't show every extreme that they name: `segment_ids`: along a stream document numbers never fall; a document has at most 1024 tokens. `page_table`: no device owns more than 32 pages of a part, and one owns exactly 32.
All inputs are finite; a program needn't handle non-finite values.
Results may differ from the reference program's by a relative error of at most 0.014.
Values may be sent and summed in bfloat16 or wider, within the bound.
A program may use at most 128 MiB of HBM per device.

```python
import math
import jax
import jax.numpy as jnp
import numpy as np
from jax import lax

D = 2048
H = 16
HD = 128
FF = 8192
LEN = 2048
STREAMS = 1
PAGE = 16
DOCS = 8
TOKENS = 2048
PAIRS = 4
HPD = 4
FF_DEV = 1024
BLOCKS = 128
CAP = 32
N_TENSOR = 8


def draw_qkv_weight(key, part):
    first_key = jax.random.fold_in(key, 0)
    drawn_all = jax.random.normal(first_key, (D, H, 3, HD), jnp.float32) / math.sqrt(D)
    return jnp.clip(drawn_all, -4.0, 4.0).reshape(D, H * 3 * HD).astype(jnp.bfloat16)


def steps_of(key, extent, shards, least, high):
    gain, own = 1.0, jax.random.fold_in(key, 6)
    for axis_at, parts in shards:
        steps = jnp.exp(jax.random.uniform(jax.random.fold_in(own, axis_at), (parts,), jnp.float32, least / len(shards), high / len(shards)))
        gain = gain * jnp.repeat(steps, extent[axis_at] // parts).reshape([-1 if axis == axis_at else 1 for axis in range(len(extent))])
    return gain


def length_profile(number_of, total, most, lean):
    portions = [(1 << 20) // math.isqrt(grade ** lean) + 1 for grade in range(2, number_of + 1)]
    spare, given = total - most - (number_of - 1), [1] * (number_of - 1)
    while spare > 0:
        candidates = [i for i in range(number_of - 1) if given[i] < most]
        pool, remaining = sum([portions[i] for i in candidates]), spare
        for i in candidates:
            more = min(most - given[i], max(1, remaining * portions[i] // pool), spare)
            given[i] = given[i] + more
            spare = spare - more
    return np.array([most] + given)


def uneven(stream_key, number_of, total, most, skew):
    if number_of == 2:
        one = jax.random.randint(stream_key, (), max(1, total - most), min(most, total - 1) + 1)
        return jnp.stack([one, total - one])
    tallies = jnp.asarray(length_profile(number_of, total, most, skew), jnp.int32)
    pairs = (number_of - 1) // 2
    giver, taker = tallies[1:1 + 2 * pairs:2], tallies[2:2 + 2 * pairs:2]
    margin = jnp.minimum(giver - 1, most - taker)
    moved = jax.random.randint(jax.random.fold_in(stream_key, 1), (pairs,), 0, 1 << 20) % (margin + 1)
    tallies = tallies.at[1:1 + 2 * pairs:2].set(giver - moved).at[2:2 + 2 * pairs:2].set(taker + moved)
    return tallies[jax.random.permutation(jax.random.fold_in(stream_key, 2), number_of)]


def shared_out(rng, own, number, rows, amount, top, reach, lean):
    order = jax.random.permutation(rng, amount)
    packed, ordinary = load_shares(amount, rows * top, reach, lean, True), load_shares(amount, rows * top, reach, lean, False)
    places = jnp.arange(amount)

    def named(sizes, rotation):
        used = int((sizes > 0).sum())
        fixed = max(1, used // 4)
        shifted = fixed + (places - fixed + rotation * (used - fixed)) % max(1, amount - fixed)
        return jnp.zeros((amount,), jnp.int32).at[order[jnp.where(places < fixed, places, shifted)]].set(jnp.asarray(sizes, jnp.int32))

    sizes = jnp.where(number % 4 == 0, named(packed, number // 4), named(ordinary, number - number // 4 - 1))
    mixed = jax.random.permutation(jax.random.fold_in(own, 3), amount)
    giver, taker = mixed[0:amount // 2 * 2:2], mixed[1:amount // 2 * 2:2]
    room = jnp.minimum(sizes[giver] - 1, reach - sizes[taker]) // 2
    room = jnp.where((giver == order[0]) | (taker == order[0]) | (sizes[taker] == 0), 0, jnp.maximum(room, 0))
    shifted = jax.random.randint(jax.random.fold_in(own, 4), (amount // 2,), 0, 1 << 20) % (room + 1)
    sizes = sizes.at[giver].add(-shifted).at[taker].add(shifted)
    items = jnp.searchsorted(jnp.cumsum(sizes), jnp.arange(rows * top), side="right").astype(jnp.int32)
    table = items.reshape(top, rows).T
    table = table[jax.random.permutation(jax.random.fold_in(own, 1), rows)]
    rotation = jax.random.randint(jax.random.fold_in(own, 2), (rows, 1), 0, top)
    return jnp.take_along_axis(table, (jnp.arange(top)[None, :] + rotation) % top, axis=1)


def load_shares(number_of, total, most, skew, full):
    portions = [(1 << 20) // math.isqrt(rank ** skew) + 1 for rank in range(1, number_of + 1)]
    largest = most if full else min(most, max(-(-total // number_of), total * portions[0] // sum(portions)))
    least = 1 if total - largest >= number_of - 1 else 0
    given, surplus = [largest] + [least] * (number_of - 1), total - largest - least * (number_of - 1)
    while surplus > 0:
        movable = [i for i in range(1, number_of) if given[i] < largest] or [i for i in range(1, number_of) if given[i] < most]
        pool, left = sum([portions[i] for i in movable]), surplus
        for i in movable:
            extra = min(most - given[i], max(1, left * portions[i] // pool), surplus)
            given[i] = given[i] + extra
            surplus = surplus - extra
    return np.array(given)


def noise(own_key, shape, scale, limit, cuts=(), held_as=jnp.bfloat16):
    entries = jax.random.normal(own_key, shape, jnp.float32) * scale
    if len(cuts) > 0:
        entries = steps_of(own_key, shape, cuts, -0.22, 0.18) * entries
    return jnp.clip(entries, min=-limit, max=limit).astype(held_as)


def setup_inputs(seed: int = 0, part: int = 0) -> dict:
    splits = jax.random.split(jax.random.key(seed), 17)
    own_keys = jax.random.split(jax.random.fold_in(splits[16], part), 17)
    hidden_in = noise(own_keys[0], (TOKENS, D), 1.0, 6.0, ((0, 8),))
    attn_gain = jnp.clip(1.0 + 0.18 * jax.random.normal(splits[1], (D,), jnp.float32), 0.1, 1.9)
    attn_shift = noise(splits[2], (D,), 0.5, 3.0, (), jnp.float32)
    qkv_weight = draw_qkv_weight(jax.random.fold_in(splits[16], 71), part)
    qkv_bias = noise(splits[4], (3 * H * HD,), 0.5, 3.0, ((0, 8),))
    out_weight = noise(splits[5], (H * HD, D), (H * HD) ** -0.5, 0.125, ((0, 8),))
    out_bias = noise(splits[6], (D,), 0.5, 3.0, (), jnp.float32)
    mlp_gain = jnp.clip(1.0 + 0.18 * jax.random.normal(splits[7], (D,), jnp.float32), 0.1, 1.9)
    mlp_shift = noise(splits[8], (D,), 0.5, 3.0, (), jnp.float32)
    up_weight = noise(splits[9], (D, FF), D ** -0.5, 0.125, ((1, 8),))
    up_bias = noise(splits[10], (FF,), 0.5, 3.0, ((0, 8),), jnp.float32)
    down_weight = noise(splits[11], (FF, D), FF ** -0.5, 0.0625, ((0, 8),))
    down_bias = noise(splits[12], (D,), 0.5, 3.0, (), jnp.float32)
    segment_ids = jax.vmap(lambda own: jnp.searchsorted(jnp.cumsum(uneven(own, DOCS, LEN, LEN // 2, 2)), jnp.arange(LEN), side="right"))(jax.random.split(own_keys[13], STREAMS)).reshape((STREAMS, LEN)).astype(jnp.int32)
    prompt_lengths = jax.random.randint(own_keys[14], (STREAMS,), LEN // 2, LEN + 1).astype(jnp.int32)
    page_table_keys = jax.random.split(jax.random.fold_in(own_keys[15], 1), BLOCKS // BLOCKS)
    page_table_turns = jax.random.permutation(jax.random.fold_in(own_keys[15], 3), BLOCKS // BLOCKS)
    page_table = jax.vmap(lambda own, number: shared_out(jax.random.fold_in(own_keys[15], 2), own, number, BLOCKS, N_TENSOR, 1, CAP, 2))(page_table_keys, page_table_turns).reshape((BLOCKS, 1))
    return dict(hidden_in=hidden_in, attn_gain=attn_gain, attn_shift=attn_shift, qkv_weight=qkv_weight, qkv_bias=qkv_bias, out_weight=out_weight, out_bias=out_bias, mlp_gain=mlp_gain, mlp_shift=mlp_shift, up_weight=up_weight, up_bias=up_bias, down_weight=down_weight, down_bias=down_bias, segment_ids=segment_ids, prompt_lengths=prompt_lengths, page_table=page_table)


def normalize(values, norm_gain, norm_shift):
    widened = values.astype(jnp.float32)
    center = lax.optimization_barrier(jnp.mean(widened, axis=-1, keepdims=True))
    spread = lax.optimization_barrier(jnp.mean(jnp.square(widened - center), axis=-1, keepdims=True))
    return (widened - center) * lax.rsqrt(spread + 1e-05) * norm_gain + norm_shift

def attend_head(queries, keys_here, values_here, segments):
    raw_scores = jnp.dot(queries, keys_here.T, preferred_element_type=jnp.float32) * (1.0 / math.sqrt(HD))
    position = jnp.arange(LEN, dtype=jnp.int32)
    allowed = (position[None, :] <= position[:, None]) & (segments[None, :] == segments[:, None])
    raw_scores = jnp.where(allowed, raw_scores, -jnp.inf)
    row_max = lax.optimization_barrier(jnp.max(raw_scores, axis=1, keepdims=True))
    expo = jnp.exp(raw_scores - row_max)
    weights = (expo / lax.optimization_barrier(jnp.sum(expo, axis=1, keepdims=True))).astype(jnp.bfloat16)
    return jnp.dot(weights, values_here, preferred_element_type=jnp.float32).astype(jnp.bfloat16)

def reference(hidden_in, attn_gain, attn_shift, qkv_weight, qkv_bias, out_weight, out_bias, mlp_gain, mlp_shift, up_weight, up_bias, down_weight, down_bias, segment_ids, prompt_lengths, page_table):
    normed = normalize(hidden_in, attn_gain, attn_shift).astype(jnp.bfloat16)
    projected = (jnp.dot(normed, qkv_weight, preferred_element_type=jnp.float32) + qkv_bias.astype(jnp.float32)).astype(jnp.bfloat16)
    grid = projected.reshape(STREAMS, LEN, H, 3, HD)

    def one_head(flat_index):
        stream_id = flat_index // H
        head_id = flat_index % H
        stream_block = lax.dynamic_index_in_dim(grid, stream_id, 0, keepdims=False)
        head_block = lax.dynamic_index_in_dim(stream_block, head_id, 1, keepdims=False)
        segments = lax.dynamic_index_in_dim(segment_ids, stream_id, 0, keepdims=False)
        return attend_head(head_block[:, 0], head_block[:, 1], head_block[:, 2], segments)
    attended = lax.map(one_head, jnp.arange(STREAMS * H, dtype=jnp.int32))
    attended = attended.reshape(STREAMS, H, LEN, HD).transpose(0, 2, 1, 3).reshape(TOKENS, H * HD)

    def head_group(running, group):
        columns = lax.dynamic_slice_in_dim(attended, group * (HPD * HD), HPD * HD, 1)
        rows_part = lax.dynamic_slice_in_dim(out_weight, group * (HPD * HD), HPD * HD, 0)
        term = jnp.dot(columns, rows_part, preferred_element_type=jnp.float32).astype(jnp.bfloat16)
        term = lax.optimization_barrier(term)
        return (running + term.astype(jnp.float32), None)
    attn_sum, _unused = lax.scan(head_group, jnp.zeros((TOKENS, D), jnp.float32), jnp.arange(PAIRS, dtype=jnp.int32))
    residual_mid = (hidden_in.astype(jnp.float32) + attn_sum + out_bias).astype(jnp.bfloat16)
    normed_mid = normalize(residual_mid, mlp_gain, mlp_shift).astype(jnp.bfloat16)
    expanded = jax.nn.gelu(jnp.dot(normed_mid, up_weight, preferred_element_type=jnp.float32) + up_bias.astype(jnp.float32), approximate=False).astype(jnp.bfloat16)

    def unit_group(running, group):
        columns = lax.dynamic_slice_in_dim(expanded, group * FF_DEV, FF_DEV, 1)
        rows_part = lax.dynamic_slice_in_dim(down_weight, group * FF_DEV, FF_DEV, 0)
        term = jnp.dot(columns, rows_part, preferred_element_type=jnp.float32).astype(jnp.bfloat16)
        term = lax.optimization_barrier(term)
        return (running + term.astype(jnp.float32), None)
    mlp_sum, _unused = lax.scan(unit_group, jnp.zeros((TOKENS, D), jnp.float32), jnp.arange(FF // FF_DEV, dtype=jnp.int32))
    layer_out = (residual_mid.astype(jnp.float32) + mlp_sum + down_bias).astype(jnp.bfloat16)
    position = jnp.arange(LEN, dtype=jnp.int32)
    live_mask = (position[None, :] < prompt_lengths[:, None]).astype(jnp.bfloat16)
    kept_rows = grid[:, :, :, 1:, :] * live_mask[:, :, None, None, None]
    page_rows = kept_rows.reshape(BLOCKS, PAGE, H * 2 * HD)
    owners = page_table[:, 0].astype(jnp.int32)
    onehot = (owners[:, None] == jnp.arange(N_TENSOR, dtype=jnp.int32)[None, :]).astype(jnp.int32)
    earlier = jnp.cumsum(onehot, axis=0) - onehot
    slot_ids = owners * CAP + lax.optimization_barrier(jnp.sum(earlier * onehot, axis=1))
    kv_pages = jnp.zeros((N_TENSOR * CAP, PAGE, H * 2 * HD), jnp.bfloat16).at[slot_ids].set(page_rows)
    return (layer_out, kv_pages)
```

```python
import functools
import math

import jax
import jax.numpy as jnp
from jax import lax
from jax.experimental import pallas as pl
from jax.experimental.pallas import tpu as pltpu
from jax.sharding import PartitionSpec as P

HD = 128
PAGE = 16
MAX_DOC = 1024
Q_BLOCK = 256
CHUNKS = 2


def normalize(values, norm_gain, norm_shift):
    widened = values.astype(jnp.float32)
    center = jnp.mean(widened, axis=-1, keepdims=True)
    spread = jnp.mean(jnp.square(widened - center), axis=-1, keepdims=True)
    return (widened - center) * lax.rsqrt(spread + 1e-05) * norm_gain + norm_shift


def attend_kernel(window, seq_len, q_ref, k_ref, v_ref, qseg_ref, kseg_ref, out_ref):
    block = pl.program_id(2)
    rows = q_ref.shape[0]
    start = jnp.clip(block * rows - MAX_DOC, 0, seq_len - window)
    start = pl.multiple_of(start, 128)
    keys = k_ref[pl.ds(start, window), :]
    values = v_ref[pl.ds(start, window), :]
    scores = lax.dot_general(
        q_ref[...], keys, (((1,), (1,)), ((), ())), preferred_element_type=jnp.float32
    ) * (1.0 / math.sqrt(HD))
    query_pos = block * rows + lax.broadcasted_iota(jnp.int32, (rows, window), 0)
    key_pos = start + lax.broadcasted_iota(jnp.int32, (rows, window), 1)
    allowed = (key_pos <= query_pos) & (qseg_ref[...] == kseg_ref[0, :, pl.ds(start, window)])
    scores = jnp.where(allowed, scores, -1e30)
    expo = jnp.exp(scores - jnp.max(scores, axis=1, keepdims=True))
    weights = (expo * (1.0 / jnp.sum(expo, axis=1, keepdims=True))).astype(jnp.bfloat16)
    out_ref[...] = jnp.dot(weights, values, preferred_element_type=jnp.float32).astype(
        jnp.bfloat16
    )


def attend(projected, segment_ids):
    streams, seq_len = segment_ids.shape
    heads = projected.shape[1] // (3 * HD)
    blocks = seq_len // Q_BLOCK
    window = min(seq_len, MAX_DOC + Q_BLOCK)
    pairs = streams * heads * seq_len * window
    return pl.pallas_call(
        functools.partial(attend_kernel, window, seq_len),
        grid=(streams, heads, blocks),
        in_specs=[
            pl.BlockSpec((Q_BLOCK, HD), lambda s, n, i: (s * blocks + i, 3 * n)),
            pl.BlockSpec((seq_len, HD), lambda s, n, i: (s, 3 * n + 1)),
            pl.BlockSpec((seq_len, HD), lambda s, n, i: (s, 3 * n + 2)),
            pl.BlockSpec((Q_BLOCK, 1), lambda s, n, i: (s * blocks + i, 0)),
            pl.BlockSpec((1, 1, seq_len), lambda s, n, i: (s, 0, 0)),
        ],
        out_specs=pl.BlockSpec((Q_BLOCK, HD), lambda s, n, i: (s * blocks + i, n)),
        out_shape=jax.ShapeDtypeStruct((streams * seq_len, heads * HD), jnp.bfloat16),
        compiler_params=pltpu.CompilerParams(vmem_limit_bytes=24 << 20),
        cost_estimate=pl.CostEstimate(
            flops=4 * pairs * HD,
            bytes_accessed=2 * projected.size * 2,
            transcendentals=pairs,
        ),
    )(
        projected,
        projected,
        projected,
        segment_ids.reshape(streams * seq_len, 1),
        segment_ids.reshape(streams, 1, seq_len),
    )


def join_pair(value, axis, position):
    devices = lax.axis_size("tensor")
    other = lax.ppermute(value, "tensor", [(source, source ^ 1) for source in range(devices)])
    first = jnp.where(position % 2 == 0, value, other)
    second = jnp.where(position % 2 == 0, other, value)
    return jnp.concatenate([first, second], axis=axis)


def pack_pages(page_rows, page_table, capacity, position):
    devices = lax.axis_size("tensor")
    pages = page_rows.shape[0]
    owners = page_table[:, 0]
    onehot = (owners[:, None] == jnp.arange(devices, dtype=jnp.int32)[None, :]).astype(jnp.int32)
    ranks = jnp.sum((jnp.cumsum(onehot, axis=0) - onehot) * onehot, axis=1)
    slot_ids = owners * capacity + ranks
    hits = slot_ids[None, :] == jnp.arange(devices * capacity, dtype=jnp.int32)[:, None]
    taken = jnp.any(hits, axis=1)
    source_page = jnp.sum(
        jnp.where(hits, jnp.arange(pages, dtype=jnp.int32)[None, :], 0), axis=1
    )
    outgoing = jnp.where(
        taken[:, None, None], jnp.take(page_rows, source_page, axis=0, mode="clip"), 0
    ).astype(jnp.bfloat16)
    outgoing = outgoing.reshape((devices, capacity) + page_rows.shape[1:])
    return [
        lax.dynamic_index_in_dim(outgoing, position ^ apart, 0, keepdims=False)
        for apart in range(devices)
    ]


def send_pages(pieces):
    devices = len(pieces)
    received = [pieces[0]]
    for apart in range(1, devices):
        hops = [(source, source ^ apart) for source in range(devices)]
        received.append(lax.ppermute(pieces[apart], "tensor", hops))
    return received


def lay_out_pages(received, position):
    devices = len(received)
    stacked = jnp.stack(received)
    origins = position ^ jnp.arange(devices, dtype=jnp.int32)
    ordered = jnp.take(stacked, origins, axis=0, mode="clip")
    return ordered.transpose(1, 2, 0, 3).reshape(ordered.shape[1], ordered.shape[2], -1)


def on_device(
    hidden_in,
    attn_gain,
    attn_shift,
    qkv_weight,
    qkv_bias,
    out_weight,
    out_bias,
    mlp_gain,
    mlp_shift,
    up_weight,
    up_bias,
    down_weight,
    down_bias,
    segment_ids,
    prompt_lengths,
    page_table,
):
    devices = lax.axis_size("tensor")
    position = lax.axis_index("tensor")
    tok_rows, width = hidden_in.shape
    total_rows = tok_rows * devices
    streams, seq_len = segment_ids.shape
    whole_heads = qkv_weight.shape[1] % (3 * HD) == 0

    normed = normalize(hidden_in, attn_gain, attn_shift).astype(jnp.bfloat16)
    if not whole_heads:
        qkv_weight = join_pair(qkv_weight, 1, position)
        qkv_bias = join_pair(qkv_bias, 0, position)
    gathered = lax.all_gather(normed, "tensor", axis=0, tiled=True)
    projected = (
        jnp.dot(gathered, qkv_weight, preferred_element_type=jnp.float32)
        + qkv_bias.astype(jnp.float32)
    ).astype(jnp.bfloat16)
    heads_here = projected.shape[1] // (3 * HD)
    attended = attend(projected, segment_ids)
    keys_vals = projected.reshape(total_rows, heads_here, 3 * HD)[:, :, HD:]
    keys_vals = keys_vals.reshape(total_rows, heads_here * 2 * HD)
    if not whole_heads:
        half = attended.shape[1] // 2
        attended = lax.dynamic_slice_in_dim(attended, position % 2 * half, half, 1)
        half = keys_vals.shape[1] // 2
        keys_vals = lax.dynamic_slice_in_dim(keys_vals, position % 2 * half, half, 1)

    blocks_total = total_rows // PAGE
    live = jnp.arange(seq_len, dtype=jnp.int32)[None, :] < prompt_lengths[:, None]
    kept_rows = jnp.where(live.reshape(total_rows, 1), keys_vals, 0).astype(jnp.bfloat16)
    pieces = pack_pages(
        kept_rows.reshape(blocks_total, PAGE, -1),
        page_table,
        2 * blocks_total // devices,
        position,
    )
    attended, pieces = lax.optimization_barrier((attended, pieces))
    received = send_pages(pieces)

    part = tok_rows // CHUNKS
    shaped = attended.reshape(devices, CHUNKS, part, attended.shape[1])
    sums = []
    for chunk in range(CHUNKS):
        rows = shaped[:, chunk].reshape(devices * part, -1)
        terms = jnp.dot(rows, out_weight, preferred_element_type=jnp.float32)
        sums.append(
            lax.psum_scatter(
                terms.astype(jnp.bfloat16), "tensor", scatter_dimension=0, tiled=True
            )
        )
    residuals, gathers = [], []
    for chunk in range(CHUNKS):
        hidden = lax.slice_in_dim(hidden_in, chunk * part, (chunk + 1) * part, axis=0)
        attn_sum = sums[chunk]
        if chunk > 0:
            attn_sum, residuals[-1], _ = lax.optimization_barrier(
                (attn_sum, residuals[-1], normed_mid)
            )
        residual_mid = (
            hidden.astype(jnp.float32) + attn_sum.astype(jnp.float32) + out_bias
        ).astype(jnp.bfloat16)
        normed_mid = normalize(residual_mid, mlp_gain, mlp_shift).astype(jnp.bfloat16)
        residuals.append(residual_mid)
        gathers.append(lax.all_gather(normed_mid, "tensor", axis=0, tiled=True))
    sums = []
    for chunk in range(CHUNKS):
        lifted = jnp.dot(gathers[chunk], up_weight, preferred_element_type=jnp.float32) + up_bias
        expanded = jax.nn.gelu(lifted, approximate=False).astype(jnp.bfloat16)
        if chunk == 0:
            expanded, received = lax.optimization_barrier((expanded, received))
        else:
            expanded = lax.optimization_barrier(expanded)
        terms = jnp.dot(expanded, down_weight, preferred_element_type=jnp.float32)
        sums.append(
            lax.psum_scatter(
                terms.astype(jnp.bfloat16), "tensor", scatter_dimension=0, tiled=True
            )
        )
    kv_pages = lay_out_pages(received, position)
    outs = [
        (residual_mid.astype(jnp.float32) + mlp_sum.astype(jnp.float32) + down_bias).astype(
            jnp.bfloat16
        )
        for residual_mid, mlp_sum in zip(residuals, sums)
    ]
    layer_out = outs[0] if CHUNKS == 1 else jnp.concatenate(outs, axis=0)
    return (layer_out, kv_pages)


def solution(mesh):
    in_specs = (
        P(("dp", "tensor"), None),
        P(),
        P(),
        P(None, "tensor"),
        P("tensor"),
        P("tensor", None),
        P(),
        P(),
        P(),
        P(None, "tensor"),
        P("tensor"),
        P("tensor", None),
        P(),
        P("dp", None),
        P("dp"),
        P("dp", None),
    )
    out_specs = (P(("dp", "tensor"), None), P(("dp", "tensor"), None, None))
    return jax.shard_map(
        on_device, mesh=mesh, in_specs=in_specs, out_specs=out_specs, check_vma=False
    )
```

```python
import functools
import math

import jax
import jax.numpy as jnp
from jax import lax
from jax.experimental import pallas as pl
from jax.experimental.pallas import tpu as pltpu
from jax.sharding import PartitionSpec as P

HD = 128
PAGE = 16
MAX_DOC = 1024
Q_BLOCK = 256
CHUNKS = 2


def normalize(values, norm_gain, norm_shift):
    widened = values.astype(jnp.float32)
    center = jnp.mean(widened, axis=-1, keepdims=True)
    spread = jnp.mean(jnp.square(widened - center), axis=-1, keepdims=True)
    return (widened - center) * lax.rsqrt(spread + 1e-05) * norm_gain + norm_shift


def attend_kernel(window, seq_len, q_ref, k_ref, v_ref, qseg_ref, kseg_ref, out_ref):
    block = pl.program_id(2)
    rows = q_ref.shape[0]
    start = jnp.clip(block * rows - MAX_DOC, 0, seq_len - window)
    start = pl.multiple_of(start, 128)
    keys = k_ref[pl.ds(start, window), :]
    values = v_ref[pl.ds(start, window), :]
    scores = lax.dot_general(
        q_ref[...], keys, (((1,), (1,)), ((), ())), preferred_element_type=jnp.float32
    ) * (1.0 / math.sqrt(HD))
    query_pos = block * rows + lax.broadcasted_iota(jnp.int32, (rows, window), 0)
    key_pos = start + lax.broadcasted_iota(jnp.int32, (rows, window), 1)
    allowed = (key_pos <= query_pos) & (qseg_ref[...] == kseg_ref[0, :, pl.ds(start, window)])
    scores = jnp.where(allowed, scores, -1e30)
    expo = jnp.exp(scores - jnp.max(scores, axis=1, keepdims=True))
    weights = (expo * (1.0 / jnp.sum(expo, axis=1, keepdims=True))).astype(jnp.bfloat16)
    out_ref[...] = jnp.dot(weights, values, preferred_element_type=jnp.float32).astype(
        jnp.bfloat16
    )


def attend(projected, segment_ids):
    streams, seq_len = segment_ids.shape
    heads = projected.shape[1] // (3 * HD)
    blocks = seq_len // Q_BLOCK
    window = min(seq_len, MAX_DOC + Q_BLOCK)
    pairs = streams * heads * seq_len * window
    return pl.pallas_call(
        functools.partial(attend_kernel, window, seq_len),
        grid=(streams, heads, blocks),
        in_specs=[
            pl.BlockSpec((Q_BLOCK, HD), lambda s, n, i: (s * blocks + i, 3 * n)),
            pl.BlockSpec((seq_len, HD), lambda s, n, i: (s, 3 * n + 1)),
            pl.BlockSpec((seq_len, HD), lambda s, n, i: (s, 3 * n + 2)),
            pl.BlockSpec((Q_BLOCK, 1), lambda s, n, i: (s * blocks + i, 0)),
            pl.BlockSpec((1, 1, seq_len), lambda s, n, i: (s, 0, 0)),
        ],
        out_specs=pl.BlockSpec((Q_BLOCK, HD), lambda s, n, i: (s * blocks + i, n)),
        out_shape=jax.ShapeDtypeStruct((streams * seq_len, heads * HD), jnp.bfloat16),
        compiler_params=pltpu.CompilerParams(vmem_limit_bytes=24 << 20),
        cost_estimate=pl.CostEstimate(
            flops=4 * pairs * HD,
            bytes_accessed=2 * projected.size * 2,
            transcendentals=pairs,
        ),
    )(
        projected,
        projected,
        projected,
        segment_ids.reshape(streams * seq_len, 1),
        segment_ids.reshape(streams, 1, seq_len),
    )


def join_pair(value, axis, position):
    devices = lax.axis_size("tensor")
    other = lax.ppermute(value, "tensor", [(source, source ^ 1) for source in range(devices)])
    first = jnp.where(position % 2 == 0, value, other)
    second = jnp.where(position % 2 == 0, other, value)
    return jnp.concatenate([first, second], axis=axis)


def pack_pages(keys_vals, live, page_table, capacity, position):
    devices = lax.axis_size("tensor")
    pages = keys_vals.shape[0] // PAGE
    owners = page_table[:, 0]
    onehot = (owners[:, None] == jnp.arange(devices, dtype=jnp.int32)[None, :]).astype(jnp.int32)
    ranks = jnp.sum((jnp.cumsum(onehot, axis=0) - onehot) * onehot, axis=1)
    slot_ids = owners * capacity + ranks
    owner_order = position ^ jnp.arange(devices, dtype=jnp.int32)
    slots = owner_order[:, None] * capacity + jnp.arange(capacity, dtype=jnp.int32)[None, :]
    hits = slot_ids[None, :] == slots.reshape(-1)[:, None]
    numbers = jnp.arange(pages, dtype=jnp.int32)
    source_page = jnp.sum(jnp.where(hits, numbers[None, :], 0), axis=1)
    live_pages = live.reshape(pages, PAGE).astype(jnp.int32)
    kept = jnp.sum(jnp.where(hits[:, :, None], live_pages[None], 0), axis=1) > 0
    page_rows = keys_vals.reshape(pages, PAGE, -1)
    taken = jnp.take(page_rows, source_page, axis=0, mode="clip")
    outgoing = jnp.where(kept[:, :, None], taken, 0).astype(jnp.bfloat16)
    return [
        lax.slice_in_dim(outgoing, apart * capacity, (apart + 1) * capacity, axis=0)
        for apart in range(devices)
    ]


def send_pages(pieces):
    devices = len(pieces)
    received = [pieces[0]]
    for apart in range(1, devices):
        hops = [(source, source ^ apart) for source in range(devices)]
        received.append(lax.ppermute(pieces[apart], "tensor", hops))
    return received


def lay_out_pages(received, position):
    devices = len(received)
    stacked = jnp.stack(received)
    origins = position ^ jnp.arange(devices, dtype=jnp.int32)
    ordered = jnp.take(stacked, origins, axis=0, mode="clip")
    return ordered.transpose(1, 2, 0, 3).reshape(ordered.shape[1], ordered.shape[2], -1)


def on_device(
    hidden_in,
    attn_gain,
    attn_shift,
    qkv_weight,
    qkv_bias,
    out_weight,
    out_bias,
    mlp_gain,
    mlp_shift,
    up_weight,
    up_bias,
    down_weight,
    down_bias,
    segment_ids,
    prompt_lengths,
    page_table,
):
    devices = lax.axis_size("tensor")
    position = lax.axis_index("tensor")
    tok_rows, width = hidden_in.shape
    total_rows = tok_rows * devices
    streams, seq_len = segment_ids.shape
    whole_heads = qkv_weight.shape[1] % (3 * HD) == 0

    normed = normalize(hidden_in, attn_gain, attn_shift).astype(jnp.bfloat16)
    if not whole_heads:
        qkv_weight = join_pair(qkv_weight, 1, position)
        qkv_bias = join_pair(qkv_bias, 0, position)
    gathered = lax.all_gather(normed, "tensor", axis=0, tiled=True)
    projected = (
        jnp.dot(gathered, qkv_weight, preferred_element_type=jnp.float32)
        + qkv_bias.astype(jnp.float32)
    ).astype(jnp.bfloat16)
    heads_here = projected.shape[1] // (3 * HD)
    keys_vals = jnp.concatenate(
        [
            lax.slice_in_dim(projected, (3 * n + 1) * HD, (3 * n + 3) * HD, axis=1)
            for n in range(heads_here)
        ],
        axis=1,
    )
    if not whole_heads:
        half = keys_vals.shape[1] // 2
        keys_vals = lax.dynamic_slice_in_dim(keys_vals, position % 2 * half, half, 1)
    live = jnp.arange(seq_len, dtype=jnp.int32)[None, :] < prompt_lengths[:, None]
    pieces = pack_pages(
        keys_vals, live, page_table, 2 * (total_rows // PAGE) // devices, position
    )
    projected, pieces = lax.optimization_barrier((projected, pieces))
    received = send_pages(pieces)
    far, step = devices // 2, devices // 8
    attended = attend(projected, segment_ids)
    if not whole_heads:
        half = attended.shape[1] // 2
        attended = lax.dynamic_slice_in_dim(attended, position % 2 * half, half, 1)
    attended, received[far : far + step] = lax.optimization_barrier(
        (attended, received[far : far + step])
    )

    part = tok_rows // CHUNKS
    shaped = attended.reshape(devices, CHUNKS, part, attended.shape[1])
    sums = []
    for chunk in range(CHUNKS):
        rows = shaped[:, chunk].reshape(devices * part, -1)
        terms = jnp.dot(rows, out_weight, preferred_element_type=jnp.float32)
        sums.append(
            lax.psum_scatter(
                terms.astype(jnp.bfloat16), "tensor", scatter_dimension=0, tiled=True
            )
        )
    residuals, gathers = [], []
    for chunk in range(CHUNKS):
        hidden = lax.slice_in_dim(hidden_in, chunk * part, (chunk + 1) * part, axis=0)
        attn_sum = sums[chunk]
        if chunk == 0:
            attn_sum, received[far + step : far + 3 * step] = lax.optimization_barrier(
                (attn_sum, received[far + step : far + 3 * step])
            )
        else:
            attn_sum, residuals[-1], received, _ = lax.optimization_barrier(
                (attn_sum, residuals[-1], received, normed_mid)
            )
        residual_mid = (
            hidden.astype(jnp.float32) + attn_sum.astype(jnp.float32) + out_bias
        ).astype(jnp.bfloat16)
        normed_mid = normalize(residual_mid, mlp_gain, mlp_shift).astype(jnp.bfloat16)
        residuals.append(residual_mid)
        gathers.append(lax.all_gather(normed_mid, "tensor", axis=0, tiled=True))
    sums = []
    for chunk in range(CHUNKS):
        lifted = jnp.dot(gathers[chunk], up_weight, preferred_element_type=jnp.float32) + up_bias
        expanded = jax.nn.gelu(lifted, approximate=False).astype(jnp.bfloat16)
        expanded = lax.optimization_barrier(expanded)
        terms = jnp.dot(expanded, down_weight, preferred_element_type=jnp.float32)
        sums.append(
            lax.psum_scatter(
                terms.astype(jnp.bfloat16), "tensor", scatter_dimension=0, tiled=True
            )
        )
    kv_pages = lay_out_pages(received, position)
    outs = [
        (residual_mid.astype(jnp.float32) + mlp_sum.astype(jnp.float32) + down_bias).astype(
            jnp.bfloat16
        )
        for residual_mid, mlp_sum in zip(residuals, sums)
    ]
    layer_out = outs[0] if CHUNKS == 1 else jnp.concatenate(outs, axis=0)
    return (layer_out, kv_pages)


def solution(mesh):
    in_specs = (
        P(("dp", "tensor"), None),
        P(),
        P(),
        P(None, "tensor"),
        P("tensor"),
        P("tensor", None),
        P(),
        P(),
        P(),
        P(None, "tensor"),
        P("tensor"),
        P("tensor", None),
        P(),
        P("dp", None),
        P("dp"),
        P("dp", None),
    )
    out_specs = (P(("dp", "tensor"), None), P(("dp", "tensor"), None, None))
    return jax.shard_map(
        on_device, mesh=mesh, in_specs=in_specs, out_specs=out_specs, check_vma=False
    )
```
